32 devices in a mesh: section: 4 (over x, core), dom: 8 (over z, y).
Axes of the slice: x: 2, y: 2, z: 4, core: 2. Of those that a mesh axis runs over, the one named last changes fastest.
Arguments:
- node_latents: bfloat16 [4, 8192, 512], P('section', 'dom'), may hold values from -6 to 6
- edge_latents: bfloat16 [4, 12288, 512], P('section', 'dom'), may hold values from -6 to 6
- entering_nodes: bfloat16 [8192, 512], P('dom'), may hold values from -6 to 6
- entering_edges: bfloat16 [12288, 512], P('dom'), may hold values from -6 to 6
- edge_first: bfloat16 [4, 1536, 512], P('section'), may hold values from -0.15625 to 0.15625
- edge_second: bfloat16 [4, 512, 512], P('section'), may hold values from -0.25 to 0.25
- edge_gain: float32 [4, 512], P('section'), may hold values from 0.1 to 1.9
- node_first: bfloat16 [4, 1024, 512], P('section'), may hold values from -0.1875 to 0.1875
- node_second: bfloat16 [4, 512, 512], P('section'), may hold values from -0.25 to 0.25
- node_gain: float32 [4, 512], P('section'), may hold values from 0.1 to 1.9
- pair_list: int32 [8, 12, 3], P('dom'), may hold values from 0 to 7, as said below
- send_list: int32 [8, 4], P('dom'), may hold values from 0 to 7, as said below
- senders: int32 [12288, 128], P('dom'), may hold values from 0 to 1, as said below
- receivers: int32 [12288, 128], P('dom'), may hold values from 0 to 1, as said below
Outputs:
- final_nodes: bfloat16 [4, 8192, 512], P('section', 'dom')
- final_edges: bfloat16 [4, 12288, 512], P('section', 'dom')
The draws below stay inside these ranges and needn't reach their ends.
Inputs may be any that keep to these rules, and one draw needn't show every extreme that they name: `pair_list`: columns 0 and 2 are node block numbers below 8, column 1 a partner code 0 to 4 (0: sender block on the same partition); every partition lists each code 1 to 4 at least once and names each of its node blocks in column 0 at least once. `send_list`: node block numbers below 8. `senders`: each row has exactly one 1. `receivers`: each row has exactly one 1.
All inputs are finite; a program needn't handle non-finite values.
Results may differ from the reference program's by a relative error of at most 0.0075.
Values may be sent and summed in bfloat16 or wider, within the bound.
No kernel may reach another device: no remote copies, remote signals or barrier semaphores. Data moves between devices by JAX's collectives and lax.ppermute only.
A program may use at most 128 MiB of HBM per device.

```python
import jax
import jax.numpy as jnp
from jax import lax

D = 512
BLOCK = 128
NODES_DEV = 1024
EDGE_BLOCKS = 12
NODES = 8192
EDGES = 12288
N_SECTION = 4
N_DOM = 8


def draw_pair_list(key, part):
    blocks = NODES_DEV // BLOCK
    number = 3 * NODES_DEV // (2 * BLOCK)

    def draw_device(device_key):
        key_recv, key_rest, key_order, key_local = jax.random.split(device_key, 4)
        receiver = (jax.random.permutation(key_recv, number) % blocks).astype(jnp.int32)
        others = jax.random.randint(key_rest, (number - 4,), 0, 5).astype(jnp.int32)
        partner_codes = jax.random.permutation(key_order, jnp.concatenate([jnp.arange(1, 5, dtype=jnp.int32), others]))
        local_block = jax.random.randint(key_local, (number,), 0, blocks).astype(jnp.int32)
        return jnp.stack([receiver, partner_codes, local_block], axis=1)
    return jax.vmap(draw_device)(jax.random.split(jax.random.fold_in(key, 5), N_DOM))


def draw_send_list(key, part):
    blocks = NODES_DEV // BLOCK
    chosen = jax.random.randint(jax.random.fold_in(key, 11), (N_DOM, 4), 0, blocks).astype(jnp.int32)
    chosen = chosen.at[0, 0].set(0)
    chosen = chosen.at[N_DOM - 1, 3].set(blocks - 1)
    return chosen


def one_hot_rows(key):
    total = 3 * NODES_DEV // (2 * BLOCK) * BLOCK * N_DOM
    column = jax.random.randint(key, (total,), 0, BLOCK)
    return (column[:, None] == jnp.arange(BLOCK)[None, :]).astype(jnp.int32)


def draw_senders(key, part):
    return one_hot_rows(jax.random.fold_in(key, 21))


def draw_receivers(key, part):
    return one_hot_rows(jax.random.fold_in(key, 22))


def shard_levels(key, dims, pieces, low, high):
    level, own = 1.0, jax.random.fold_in(key, 6)
    for position, shards_of in pieces:
        steps = jnp.exp(jax.random.uniform(jax.random.fold_in(own, position), (shards_of,), jnp.float32, low / len(pieces), high / len(pieces)))
        level = level * jnp.repeat(steps, dims[position] // shards_of).reshape([-1 if axis == position else 1 for axis in range(len(dims))])
    return level


def bell_draw(key, extent, deviation, reach, shards=(), kind=jnp.bfloat16):
    loudness = shard_levels(key, extent, shards, -0.22, 0.18) if shards else 1.0
    values = jax.random.normal(key, extent, jnp.float32) * deviation * loudness
    return jnp.minimum(jnp.maximum(values, -reach), reach).astype(kind)


def setup_inputs(seed: int = 0) -> dict:
    key_list = jax.random.split(jax.random.key(seed), 15)
    return {
        "node_latents": bell_draw(key_list[0], (N_SECTION, NODES, D), 1.0, 6.0, ((0, 4), (1, 8))),
        "edge_latents": bell_draw(key_list[1], (N_SECTION, EDGES, D), 1.0, 6.0, ((0, 4), (1, 8))),
        "entering_nodes": bell_draw(key_list[2], (NODES, D), 1.0, 6.0, ((0, 8),)),
        "entering_edges": bell_draw(key_list[3], (EDGES, D), 1.0, 6.0, ((0, 8),)),
        "edge_first": bell_draw(key_list[4], (N_SECTION, 3 * D, D), (3 * D) ** -0.5, 0.15625, ((0, 4),)),
        "edge_second": bell_draw(key_list[5], (N_SECTION, D, D), D ** -0.5, 0.25, ((0, 4),)),
        "edge_gain": jnp.clip(1.0 + 0.18 * jax.random.normal(key_list[6], (N_SECTION, D), jnp.float32), 0.1, 1.9),
        "node_first": bell_draw(key_list[7], (N_SECTION, 2 * D, D), (2 * D) ** -0.5, 0.1875, ((0, 4),)),
        "node_second": bell_draw(key_list[8], (N_SECTION, D, D), D ** -0.5, 0.25, ((0, 4),)),
        "node_gain": jnp.clip(1.0 + 0.18 * jax.random.normal(key_list[9], (N_SECTION, D), jnp.float32), 0.1, 1.9),
        "pair_list": draw_pair_list(jax.random.fold_in(key_list[14], 71), 0),
        "send_list": draw_send_list(jax.random.fold_in(key_list[14], 71), 0),
        "senders": draw_senders(jax.random.fold_in(key_list[14], 71), 0),
        "receivers": draw_receivers(jax.random.fold_in(key_list[14], 71), 0),
    }


partner_offsets = (1, -1, 2, -2)
epsilon = 1e-05
highest = lax.Precision.HIGHEST

def layer_norm(values, gain):
    centred = values - lax.optimization_barrier(jnp.mean(values, axis=-1, keepdims=True))
    spread = lax.optimization_barrier(jnp.mean(centred * centred, axis=-1, keepdims=True))
    return centred * lax.rsqrt(spread + epsilon) * gain

def product_wide(left, right):
    return jnp.dot(left.astype(jnp.float32), right.astype(jnp.float32), precision=highest)

def batched(form, left, right):
    return jnp.einsum(form, left.astype(jnp.float32), right.astype(jnp.float32), precision=highest)

def selector(index, number):
    return (index[:, None] == jnp.arange(number, dtype=jnp.int32)[None, :]).astype(jnp.float32)

def edge_part(node_rows, edge_rows, incoming, pairs, send_mat, recv_mat, edge_first, edge_second, edge_gain):
    blocks = NODES_DEV // BLOCK
    rows_all = EDGE_BLOCKS * BLOCK
    own_blocks = node_rows.reshape(blocks, BLOCK, D)
    lookup = jnp.concatenate([own_blocks, incoming], axis=0)
    partner_codes = pairs[:, 1]
    source = jnp.where(partner_codes == 0, pairs[:, 2], blocks + partner_codes - 1).astype(jnp.int32)
    sender_blocks = lookup[source]
    receiver_blocks = own_blocks[pairs[:, 0]]
    from_send = batched('kei,kid->ked', send_mat, sender_blocks).astype(jnp.bfloat16)
    from_recv = batched('kei,kid->ked', recv_mat, receiver_blocks).astype(jnp.bfloat16)
    first_layer = product_wide(edge_rows, edge_first[:D])
    first_layer = first_layer + product_wide(from_send.reshape(rows_all, D), edge_first[D:2 * D])
    first_layer = first_layer + product_wide(from_recv.reshape(rows_all, D), edge_first[2 * D:])
    hidden = jnp.maximum(first_layer, 0.0).astype(jnp.bfloat16)
    message = layer_norm(product_wide(hidden, edge_second), edge_gain)
    message_low = message.astype(jnp.bfloat16)
    new_edges = (edge_rows.astype(jnp.float32) + message).astype(jnp.bfloat16)
    blocked = message_low.reshape(EDGE_BLOCKS, BLOCK, D)
    at_send = batched('kei,ked->kid', send_mat, blocked)
    at_recv = batched('kei,ked->kid', recv_mat, blocked)
    block_sums = batched('kn,kbd->nbd', selector(pairs[:, 0], blocks + 4), at_recv)
    block_sums = block_sums + batched('kn,kbd->nbd', selector(source, blocks + 4), at_send)
    return (new_edges, block_sums[:blocks], block_sums[blocks:].astype(jnp.bfloat16))

def node_part(node_rows, own_sums, returned, sends, node_first, node_second, node_gain):
    blocks = NODES_DEV // BLOCK
    gathered = own_sums + batched('jn,jbd->nbd', selector(sends, blocks), returned)
    summed = gathered.reshape(NODES_DEV, D).astype(jnp.bfloat16)
    first_layer = product_wide(node_rows, node_first[:D]) + product_wide(summed, node_first[D:])
    hidden = jnp.maximum(first_layer, 0.0).astype(jnp.bfloat16)
    update = layer_norm(product_wide(hidden, node_second), node_gain)
    return (node_rows.astype(jnp.float32) + update).astype(jnp.bfloat16)

def whole_layer(nodes, edges, weights, pair_list, send_list, send_mats, recv_mats):
    edge_first, edge_second, edge_gain, node_first, node_second, node_gain = weights
    blocks = NODES_DEV // BLOCK
    own = nodes.reshape(N_DOM, blocks, BLOCK, D)
    outgoing = jax.vmap(lambda blocks_of, chosen: blocks_of[chosen])(own, send_list)
    incoming = jnp.stack([jnp.roll(outgoing[:, offset_slot], partner_offsets[offset_slot], axis=0) for offset_slot in range(4)], axis=1)
    new_edges, own_sums, partials = jax.vmap(edge_part, in_axes=(0, 0, 0, 0, 0, 0, None, None, None))(nodes, edges, incoming, pair_list, send_mats, recv_mats, edge_first, edge_second, edge_gain)
    returned = jnp.stack([jnp.roll(partials[:, offset_slot], -partner_offsets[offset_slot], axis=0) for offset_slot in range(4)], axis=1)
    new_nodes = jax.vmap(node_part, in_axes=(0, 0, 0, 0, None, None, None))(nodes, own_sums, returned, send_list, node_first, node_second, node_gain)
    return (new_nodes, new_edges)

def reference(node_latents, edge_latents, entering_nodes, entering_edges, edge_first, edge_second, edge_gain, node_first, node_second, node_gain, pair_list, send_list, senders, receivers):
    edge_count = EDGE_BLOCKS * BLOCK
    send_mats = senders.reshape(N_DOM, EDGE_BLOCKS, BLOCK, BLOCK)
    recv_mats = receivers.reshape(N_DOM, EDGE_BLOCKS, BLOCK, BLOCK)

    def run_layer(section, nodes, edges):
        weights = (edge_first[section], edge_second[section], edge_gain[section], node_first[section], node_second[section], node_gain[section])
        new_nodes, new_edges = whole_layer(nodes.reshape(N_DOM, NODES_DEV, D), edges.reshape(N_DOM, edge_count, D), weights, pair_list, send_list, send_mats, recv_mats)
        return (new_nodes.reshape(NODES, D), new_edges.reshape(EDGES, D))
    ticked = [run_layer(section, node_latents[section], edge_latents[section]) for section in range(N_SECTION)]
    inputs = [(entering_nodes, entering_edges)] + ticked[:-1]
    results = [run_layer(section, inputs[section][0], inputs[section][1]) for section in range(N_SECTION)]
    final_nodes = jnp.stack([entry[0] for entry in results], axis=0)
    final_edges = jnp.stack([entry[1] for entry in results], axis=0)
    return (final_nodes, final_edges)
```

```python
import functools

import jax
import jax.numpy as jnp
from jax import lax
from jax.experimental import pallas as pl
from jax.experimental.pallas import tpu as pltpu
from jax.sharding import PartitionSpec as P

partner_offsets = (1, -1, 2, -2)
epsilon = 1e-05
f32 = jnp.float32
bf16 = jnp.bfloat16
VMEM = pl.BlockSpec(memory_space=pltpu.VMEM)
SMEM = pl.BlockSpec(memory_space=pltpu.SMEM)


def passed_along(block, axis, distance):
    devices = range(lax.axis_size(axis))
    route = [((i - distance) % len(devices), i) for i in devices]
    return lax.ppermute(block, axis, route)


def from_behind(value, axis):
    count = lax.axis_size(axis)
    return lax.ppermute(value, axis, [(source, source + 1) for source in range(count - 1)])


def layer_norm(values, gain):
    centred = values - jnp.mean(values, axis=-1, keepdims=True)
    spread = jnp.mean(centred * centred, axis=-1, keepdims=True)
    return centred * lax.rsqrt(spread + epsilon) * gain


def product(left, right):
    return jnp.dot(left, right, preferred_element_type=f32)


def call(kernel, name, outs, ins, operands, scratch=(), flops=0, moved=0):
    return pl.pallas_call(
        kernel,
        name=name,
        out_shape=outs,
        in_specs=ins,
        out_specs=jax.tree.map(lambda _: VMEM, outs),
        scratch_shapes=list(scratch),
        compiler_params=pltpu.CompilerParams(vmem_limit_bytes=60 << 20),
        cost_estimate=pl.CostEstimate(flops=flops, bytes_accessed=moved, transcendentals=0),
    )(*operands)


def shape(dims, kind):
    return jax.ShapeDtypeStruct(dims, kind)


def pick_kernel(sends, nodes, *outs):
    rows = outs[0].shape[0]
    for slot in range(4):
        start = pl.multiple_of(sends[slot] * rows, rows)
        outs[slot][...] = nodes[pl.ds(start, rows), :]


def pick_select_kernel(flag, sends, entering, moved, nodes, *outs):
    rows = outs[0].shape[0]

    @pl.when(flag[0] == 0)
    def _():
        nodes[...] = entering[...]

    @pl.when(flag[0] != 0)
    def _():
        nodes[...] = moved[...]

    for slot in range(4):
        start = pl.multiple_of(sends[slot] * rows, rows)
        outs[slot][...] = nodes[pl.ds(start, rows), :]


def ends_kernel(senders, receivers, ends, flipped):
    rows = senders.shape[1]
    for block in range(senders.shape[0] // rows):
        here = pl.ds(block * rows, rows)
        for side, source in enumerate((senders, receivers)):
            part = source[here, :].astype(f32)
            ends[here, side * rows : (side + 1) * rows] = part.astype(bf16)
            flipped[pl.ds((2 * block + side) * rows, rows), :] = part.T.astype(bf16)


def project_kernel(edges, nodes, edge_first, base, sent, received):
    width = nodes.shape[1]
    base[...] = product(edges[...], edge_first[:width, :])
    sent[...] = product(nodes[...], edge_first[width : 2 * width, :]).astype(bf16)
    received[...] = product(nodes[...], edge_first[2 * width :, :]).astype(bf16)


def project_select_kernel(flag, entering, moved, nodes, edge_first, edges, base, sent, received):
    @pl.when(flag[0] == 0)
    def _():
        edges[...] = entering[...]

    @pl.when(flag[0] != 0)
    def _():
        edges[...] = moved[...]

    project_kernel(edges, nodes, edge_first, base, sent, received)


def edge_kernel(
    pairs,
    in_one,
    in_two,
    in_three,
    in_four,
    base,
    sent,
    received,
    ends,
    flipped,
    edges,
    edge_first,
    edge_second,
    gain,
    new_edges,
    own,
    out_one,
    out_two,
    out_three,
    out_four,
    lookup,
    sums,
):
    rows, width = in_one.shape
    blocks = sent.shape[0] // rows
    number = edges.shape[0] // rows
    lookup[: blocks * rows, :] = sent[...]
    middle = edge_first[width : 2 * width, :]
    for slot, block in enumerate((in_one, in_two, in_three, in_four)):
        lookup[(blocks + slot) * rows : (blocks + slot + 1) * rows, :] = product(
            block[...], middle
        ).astype(bf16)
    sums[...] = jnp.zeros_like(sums)
    group = 4 if number % 4 == 0 else 1
    for first in range(0, number, group):
        hidden = []
        places = []
        for block in range(first, first + group):
            code = pairs[block, 1]
            source = jnp.where(code == 0, pairs[block, 2], blocks + code - 1)
            source = pl.multiple_of(source * rows, rows)
            target = pl.multiple_of(pairs[block, 0] * rows, rows)
            places.append((source, target))
            both = jnp.concatenate(
                [lookup[pl.ds(source, rows), :], received[pl.ds(target, rows), :]], axis=0
            )
            here = slice(block * rows, (block + 1) * rows)
            summed = base[here, :] + product(ends[here, :], both)
            hidden.append(jnp.maximum(summed, 0.0).astype(bf16))
        message = layer_norm(product(jnp.concatenate(hidden, axis=0), edge_second[...]), gain[...])
        span = slice(first * rows, (first + group) * rows)
        new_edges[span, :] = (edges[span, :].astype(f32) + message).astype(bf16)
        low = message.astype(bf16)
        for index, (source, target) in enumerate(places):
            block = first + index
            spread = product(
                flipped[2 * block * rows : 2 * (block + 1) * rows, :],
                low[index * rows : (index + 1) * rows, :],
            )
            sums[pl.ds(source, rows), :] += spread[:rows, :]
            sums[pl.ds(target, rows), :] += spread[rows:, :]
    own[...] = sums[: blocks * rows, :]
    for slot, out in enumerate((out_one, out_two, out_three, out_four)):
        out[...] = sums[(blocks + slot) * rows : (blocks + slot + 1) * rows, :].astype(bf16)


def ready_kernel(nodes, node_first, partial):
    partial[...] = product(nodes[...], node_first[: nodes.shape[1], :])


def node_kernel(
    sends,
    back_one,
    back_two,
    back_three,
    back_four,
    own,
    partial,
    nodes,
    node_first,
    node_second,
    gain,
    new_nodes,
    total,
):
    rows, width = back_one.shape
    total[...] = own[...]
    for slot, block in enumerate((back_one, back_two, back_three, back_four)):
        start = pl.multiple_of(sends[slot] * rows, rows)
        total[pl.ds(start, rows), :] += block[...].astype(f32)
    hidden = partial[...] + product(total[...].astype(bf16), node_first[width:, :])
    hidden = jnp.maximum(hidden, 0.0).astype(bf16)
    update = layer_norm(product(hidden, node_second[...]), gain[...])
    new_nodes[...] = (nodes[...].astype(f32) + update).astype(bf16)


def local(
    node_latents,
    edge_latents,
    entering_nodes,
    entering_edges,
    edge_first,
    edge_second,
    edge_gain,
    node_first,
    node_second,
    node_gain,
    pair_list,
    send_list,
    senders,
    receivers,
):
    edge_first, edge_second, node_first, node_second = (
        edge_first[0],
        edge_second[0],
        node_first[0],
        node_second[0],
    )
    pairs = pair_list[0]
    sends = send_list[0]
    flag = lax.axis_index("section").astype(jnp.int32).reshape(1)
    node_rows, width = entering_nodes.shape
    edge_rows = entering_edges.shape[0]
    rows = senders.shape[1]
    block = shape((rows, width), bf16)
    ends, flipped = None, None

    def tick(nodes, edges, picked, ends, flipped, projected):
        incoming = [passed_along(picked[i], "dom", partner_offsets[i]) for i in range(4)]
        if ends is None:
            ends, flipped = call(
                ends_kernel,
                "ends",
                (shape((edge_rows, 2 * rows), bf16), shape((2 * edge_rows, rows), bf16)),
                [VMEM] * 2,
                (senders, receivers),
                flops=10**8,
                moved=3 << 20,
            )
        edges, base, sent, received = projected(nodes)
        new_edges, own, *partials = call(
            edge_kernel,
            "edge",
            (
                shape((edge_rows, width), bf16),
                shape((node_rows, width), f32),
                block,
                block,
                block,
                block,
            ),
            [SMEM] + [VMEM] * 13,
            (
                pairs,
                *incoming,
                base,
                sent,
                received,
                ends,
                flipped,
                edges,
                edge_first,
                edge_second,
                edge_gain,
            ),
            scratch=(
                pltpu.VMEM((node_rows + 4 * rows, width), bf16),
                pltpu.VMEM((node_rows + 4 * rows, width), f32),
            ),
            flops=4 * 10**9,
            moved=12 << 20,
        )
        returned = [passed_along(partials[i], "dom", -partner_offsets[i]) for i in range(4)]
        partial = call(
            ready_kernel,
            "ready",
            shape((node_rows, width), f32),
            [VMEM] * 2,
            (nodes, node_first),
            flops=2 * node_rows * width * width,
            moved=3 << 20,
        )
        new_nodes = call(
            node_kernel,
            "node",
            shape((node_rows, width), bf16),
            [SMEM] + [VMEM] * 10,
            (
                sends,
                *returned,
                own,
                partial,
                nodes,
                node_first,
                node_second,
                node_gain,
            ),
            scratch=(pltpu.VMEM((node_rows, width), f32),),
            flops=4 * node_rows * width * width,
            moved=8 << 20,
        )
        return new_nodes, new_edges, ends, flipped

    project_outs = (
        shape((edge_rows, width), f32),
        shape((node_rows, width), bf16),
        shape((node_rows, width), bf16),
    )
    project_cost = dict(flops=2 * (edge_rows + 2 * node_rows) * width * width, moved=9 << 20)
    nodes, edges = node_latents[0], edge_latents[0]
    picked = call(pick_kernel, "pick", (block,) * 4, [SMEM, VMEM], (sends, nodes))

    def project_now(nodes):
        return edges, *call(
            project_kernel,
            "project",
            project_outs,
            [VMEM] * 3,
            (edges, nodes, edge_first),
            **project_cost,
        )

    nodes, new_edges, ends, flipped = tick(nodes, edges, picked, None, None, project_now)
    moved_nodes = from_behind(nodes, "section")
    moved_edges = from_behind(new_edges, "section")
    nodes, *picked = call(
        pick_select_kernel,
        "pick_select",
        (shape((node_rows, width), bf16),) + (block,) * 4,
        [SMEM] * 2 + [VMEM] * 2,
        (flag, sends, entering_nodes, moved_nodes),
    )

    def project_later(nodes):
        return call(
            project_select_kernel,
            "project_select",
            (shape((edge_rows, width), bf16),) + project_outs,
            [SMEM] + [VMEM] * 4,
            (flag, entering_edges, moved_edges, nodes, edge_first),
            **project_cost,
        )

    nodes, new_edges, _, _ = tick(nodes, None, picked, ends, flipped, project_later)
    return (nodes[None], new_edges[None])


def solution(mesh):
    placed = (
        P("section", "dom", None),
        P("section", "dom", None),
        P("dom", None),
        P("dom", None),
        P("section", None, None),
        P("section", None, None),
        P("section", None),
        P("section", None, None),
        P("section", None, None),
        P("section", None),
        P("dom", None, None),
        P("dom", None),
        P("dom", None),
        P("dom", None),
    )
    return jax.shard_map(
        local,
        mesh=mesh,
        in_specs=placed,
        out_specs=(P("section", "dom", None), P("section", "dom", None)),
        check_vma=False,
    )
```

```python
import functools

import jax
import jax.numpy as jnp
from jax import lax
from jax.experimental import pallas as pl
from jax.experimental.pallas import tpu as pltpu
from jax.sharding import PartitionSpec as P

partner_offsets = (1, -1, 2, -2)
epsilon = 1e-05
f32 = jnp.float32
bf16 = jnp.bfloat16
VMEM = pl.BlockSpec(memory_space=pltpu.VMEM)
SMEM = pl.BlockSpec(memory_space=pltpu.SMEM)


def passed_along(block, axis, distance):
    devices = range(lax.axis_size(axis))
    route = [((i - distance) % len(devices), i) for i in devices]
    return lax.ppermute(block, axis, route)


def from_behind(value, axis):
    count = lax.axis_size(axis)
    return lax.ppermute(value, axis, [(source, source + 1) for source in range(count - 1)])


def layer_norm(values, gain):
    centred = values - jnp.mean(values, axis=-1, keepdims=True)
    spread = jnp.mean(centred * centred, axis=-1, keepdims=True)
    return centred * lax.rsqrt(spread + epsilon) * gain


def product(left, right):
    return jnp.dot(left, right, preferred_element_type=f32)


def call(kernel, name, outs, ins, operands, scratch=(), flops=0, moved=0):
    return pl.pallas_call(
        kernel,
        name=name,
        out_shape=outs,
        in_specs=ins,
        out_specs=jax.tree.map(lambda _: VMEM, outs),
        scratch_shapes=list(scratch),
        compiler_params=pltpu.CompilerParams(vmem_limit_bytes=24 << 20),
        cost_estimate=pl.CostEstimate(flops=flops, bytes_accessed=moved, transcendentals=0),
    )(*operands)


def shape(dims, kind):
    return jax.ShapeDtypeStruct(dims, kind)


def pick_kernel(sends, nodes, *outs):
    rows = outs[0].shape[0]
    for slot in range(4):
        start = pl.multiple_of(sends[slot] * rows, rows)
        outs[slot][...] = nodes[pl.ds(start, rows), :]


def pick_select_kernel(flag, sends, entering, moved, nodes, *outs):
    rows = outs[0].shape[0]

    @pl.when(flag[0] == 0)
    def _():
        nodes[...] = entering[...]

    @pl.when(flag[0] != 0)
    def _():
        nodes[...] = moved[...]

    for slot in range(4):
        start = pl.multiple_of(sends[slot] * rows, rows)
        outs[slot][...] = nodes[pl.ds(start, rows), :]


def ends_kernel(senders, receivers, ends, flipped):
    rows = senders.shape[1]
    for block in range(senders.shape[0] // rows):
        here = pl.ds(block * rows, rows)
        for side, source in enumerate((senders, receivers)):
            part = source[here, :].astype(f32)
            ends[here, side * rows : (side + 1) * rows] = part.astype(bf16)
            flipped[pl.ds((2 * block + side) * rows, rows), :] = part.T.astype(bf16)


def project_kernel(edges, nodes, edge_first, base, sent, received):
    width = nodes.shape[1]
    base[...] = product(edges[...], edge_first[:width, :])
    sent[...] = product(nodes[...], edge_first[width : 2 * width, :]).astype(bf16)
    received[...] = product(nodes[...], edge_first[2 * width :, :]).astype(bf16)


def project_select_kernel(flag, entering, moved, nodes, edge_first, edges, base, sent, received):
    @pl.when(flag[0] == 0)
    def _():
        edges[...] = entering[...]

    @pl.when(flag[0] != 0)
    def _():
        edges[...] = moved[...]

    project_kernel(edges, nodes, edge_first, base, sent, received)


def edge_kernel(
    pairs,
    in_one,
    in_two,
    in_three,
    in_four,
    base,
    sent,
    received,
    ends,
    flipped,
    edges,
    edge_first,
    edge_second,
    gain,
    new_edges,
    own,
    out_one,
    out_two,
    out_three,
    out_four,
    lookup,
    sums,
):
    rows, width = in_one.shape
    blocks = sent.shape[0] // rows
    number = edges.shape[0] // rows
    lookup[: blocks * rows, :] = sent[...]
    middle = edge_first[width : 2 * width, :]
    for slot, block in enumerate((in_one, in_two, in_three, in_four)):
        lookup[(blocks + slot) * rows : (blocks + slot + 1) * rows, :] = product(
            block[...], middle
        ).astype(bf16)
    sums[...] = jnp.zeros_like(sums)
    group = 4 if number % 4 == 0 else 1
    for first in range(0, number, group):
        hidden = []
        places = []
        for block in range(first, first + group):
            code = pairs[block, 1]
            source = jnp.where(code == 0, pairs[block, 2], blocks + code - 1)
            source = pl.multiple_of(source * rows, rows)
            target = pl.multiple_of(pairs[block, 0] * rows, rows)
            places.append((source, target))
            both = jnp.concatenate(
                [lookup[pl.ds(source, rows), :], received[pl.ds(target, rows), :]], axis=0
            )
            here = slice(block * rows, (block + 1) * rows)
            summed = base[here, :] + product(ends[here, :], both)
            hidden.append(jnp.maximum(summed, 0.0).astype(bf16))
        message = layer_norm(product(jnp.concatenate(hidden, axis=0), edge_second[...]), gain[...])
        span = slice(first * rows, (first + group) * rows)
        new_edges[span, :] = (edges[span, :].astype(f32) + message).astype(bf16)
        low = message.astype(bf16)
        for index, (source, target) in enumerate(places):
            block = first + index
            spread = product(
                flipped[2 * block * rows : 2 * (block + 1) * rows, :],
                low[index * rows : (index + 1) * rows, :],
            )
            sums[pl.ds(source, rows), :] += spread[:rows, :]
            sums[pl.ds(target, rows), :] += spread[rows:, :]
    own[...] = sums[: blocks * rows, :]
    for slot, out in enumerate((out_one, out_two, out_three, out_four)):
        out[...] = sums[(blocks + slot) * rows : (blocks + slot + 1) * rows, :].astype(bf16)


def ready_kernel(nodes, node_first, partial):
    partial[...] = product(nodes[...], node_first[: nodes.shape[1], :])


def node_kernel(
    sends,
    back_one,
    back_two,
    back_three,
    back_four,
    own,
    partial,
    nodes,
    node_first,
    node_second,
    gain,
    new_nodes,
    total,
):
    rows, width = back_one.shape
    total[...] = own[...]
    for slot, block in enumerate((back_one, back_two, back_three, back_four)):
        start = pl.multiple_of(sends[slot] * rows, rows)
        total[pl.ds(start, rows), :] += block[...].astype(f32)
    hidden = partial[...] + product(total[...].astype(bf16), node_first[width:, :])
    hidden = jnp.maximum(hidden, 0.0).astype(bf16)
    update = layer_norm(product(hidden, node_second[...]), gain[...])
    new_nodes[...] = (nodes[...].astype(f32) + update).astype(bf16)


def local(
    node_latents,
    edge_latents,
    entering_nodes,
    entering_edges,
    edge_first,
    edge_second,
    edge_gain,
    node_first,
    node_second,
    node_gain,
    pair_list,
    send_list,
    senders,
    receivers,
):
    edge_first, edge_second, node_first, node_second = (
        edge_first[0],
        edge_second[0],
        node_first[0],
        node_second[0],
    )
    pairs = pair_list[0]
    sends = send_list[0]
    flag = lax.axis_index("section").astype(jnp.int32).reshape(1)
    node_rows, width = entering_nodes.shape
    edge_rows = entering_edges.shape[0]
    rows = senders.shape[1]
    block = shape((rows, width), bf16)
    ends, flipped = None, None

    def tick(nodes, edges, picked, ends, flipped, projected):
        incoming = [passed_along(picked[i], "dom", partner_offsets[i]) for i in range(4)]
        if ends is None:
            ends, flipped = call(
                ends_kernel,
                "ends",
                (shape((edge_rows, 2 * rows), bf16), shape((2 * edge_rows, rows), bf16)),
                [VMEM] * 2,
                (senders, receivers),
                flops=10**8,
                moved=3 << 20,
            )
        edges, base, sent, received = projected(nodes)
        new_edges, own, *partials = call(
            edge_kernel,
            "edge",
            (
                shape((edge_rows, width), bf16),
                shape((node_rows, width), f32),
                block,
                block,
                block,
                block,
            ),
            [SMEM] + [VMEM] * 13,
            (
                pairs,
                *incoming,
                base,
                sent,
                received,
                ends,
                flipped,
                edges,
                edge_first,
                edge_second,
                edge_gain,
            ),
            scratch=(
                pltpu.VMEM((node_rows + 4 * rows, width), bf16),
                pltpu.VMEM((node_rows + 4 * rows, width), f32),
            ),
            flops=4 * 10**9,
            moved=12 << 20,
        )
        returned = [passed_along(partials[i], "dom", -partner_offsets[i]) for i in range(4)]
        partial = call(
            ready_kernel,
            "ready",
            shape((node_rows, width), f32),
            [VMEM] * 2,
            (nodes, node_first),
            flops=2 * node_rows * width * width,
            moved=3 << 20,
        )
        new_nodes = call(
            node_kernel,
            "node",
            shape((node_rows, width), bf16),
            [SMEM] + [VMEM] * 10,
            (
                sends,
                *returned,
                own,
                partial,
                nodes,
                node_first,
                node_second,
                node_gain,
            ),
            scratch=(pltpu.VMEM((node_rows, width), f32),),
            flops=4 * node_rows * width * width,
            moved=8 << 20,
        )
        return new_nodes, new_edges, ends, flipped

    project_outs = (
        shape((edge_rows, width), f32),
        shape((node_rows, width), bf16),
        shape((node_rows, width), bf16),
    )
    project_cost = dict(flops=2 * (edge_rows + 2 * node_rows) * width * width, moved=9 << 20)
    nodes, edges = node_latents[0], edge_latents[0]
    picked = call(pick_kernel, "pick", (block,) * 4, [SMEM, VMEM], (sends, nodes))

    def project_now(nodes):
        return edges, *call(
            project_kernel,
            "project",
            project_outs,
            [VMEM] * 3,
            (edges, nodes, edge_first),
            **project_cost,
        )

    nodes, new_edges, ends, flipped = tick(nodes, edges, picked, None, None, project_now)
    moved_nodes = from_behind(nodes, "section")
    moved_edges = from_behind(new_edges, "section")
    nodes, *picked = call(
        pick_select_kernel,
        "pick_select",
        (shape((node_rows, width), bf16),) + (block,) * 4,
        [SMEM] * 2 + [VMEM] * 2,
        (flag, sends, entering_nodes, moved_nodes),
    )

    def project_later(nodes):
        return call(
            project_select_kernel,
            "project_select",
            (shape((edge_rows, width), bf16),) + project_outs,
            [SMEM] + [VMEM] * 4,
            (flag, entering_edges, moved_edges, nodes, edge_first),
            **project_cost,
        )

    nodes, new_edges, _, _ = tick(nodes, None, picked, ends, flipped, project_later)
    return (nodes[None], new_edges[None])


def solution(mesh):
    placed = (
        P("section", "dom", None),
        P("section", "dom", None),
        P("dom", None),
        P("dom", None),
        P("section", None, None),
        P("section", None, None),
        P("section", None),
        P("section", None, None),
        P("section", None, None),
        P("section", None),
        P("dom", None, None),
        P("dom", None),
        P("dom", None),
        P("dom", None),
    )
    return jax.shard_map(
        local,
        mesh=mesh,
        in_specs=placed,
        out_specs=(P("section", "dom", None), P("section", "dom", None)),
        check_vma=False,
    )
```

```python
import jax
import jax.numpy as jnp
from jax import lax
from jax.experimental import pallas as pl
from jax.experimental.pallas import tpu as pltpu
from jax.sharding import PartitionSpec as P


partner_offsets = (1, -1, 2, -2)
partners = len(partner_offsets)
epsilon = 1e-05
f32 = jnp.float32
bf16 = jnp.bfloat16
VMEM = pl.BlockSpec(memory_space=pltpu.VMEM)
SMEM = pl.BlockSpec(memory_space=pltpu.SMEM)
HBM = pl.BlockSpec(memory_space=pltpu.HBM)
group = 3


def rotated(block, axis, distance):
    devices = range(lax.axis_size(axis))
    route = [((i - distance) % len(devices), i) for i in devices]
    return lax.ppermute(block, axis, route)


def layer_norm(values, gain):
    centred = values - jnp.mean(values, axis=-1, keepdims=True)
    spread = jnp.mean(centred * centred, axis=-1, keepdims=True)
    return centred * lax.rsqrt(spread + epsilon) * gain


def product(left, right):
    return jnp.dot(left, right, preferred_element_type=f32)


def shape(dims, kind):
    return jax.ShapeDtypeStruct(dims, kind)


def call(kernel, ins, outs, scratch=(), copies=0, aliases=None, flops=0, moved=0):
    specs = {"v": VMEM, "s": SMEM, "h": HBM}
    scratch = list(scratch)
    if copies:
        scratch.append(pltpu.SemaphoreType.DMA((copies,)))
    step = pl.pallas_call(
        kernel,
        out_shape=tuple(out for _, out in outs),
        in_specs=[specs[place] for place, _ in ins],
        out_specs=tuple(specs[place] for place, _ in outs),
        scratch_shapes=scratch,
        input_output_aliases=aliases or {},
        compiler_params=pltpu.CompilerParams(vmem_limit_bytes=24 << 20),
        cost_estimate=pl.CostEstimate(flops=flops, bytes_accessed=moved, transcendentals=0),
    )
    values = [
            pltpu.with_memory_space_constraint(value, pltpu.HBM) if place == "h" else value
            for place, value in ins
    ]
    return step(*values)


def started(pairs, sems, first=0):
    copies = [
        pltpu.make_async_copy(source, target, sems.at[first + i])
        for i, (source, target) in enumerate(pairs)
    ]
    for copy in copies:
        copy.start()
    return copies


def finish(copies):
    for copy in copies:
        copy.wait()


def aligned(index, rows):
    return pl.ds(pl.multiple_of(index * rows, rows), rows)


def span(index, rows):
    return pl.ds(index * rows, rows)


def plan_kernel(sends_far, pairs_far, nodes, plan, front, back, *rest):
    outs, (near, sends, pairs, sems) = rest[:partners], rest[partners:]
    rows = outs[0].shape[0]
    blocks = nodes.shape[0] // rows
    number = pairs.shape[2]
    copies = started([(sends_far, sends), (nodes, near), (pairs_far, pairs)], sems)
    copies[0].wait()
    chosen = [sends[0, i] for i in range(partners)]
    used = []
    for block in range(blocks):
        hit = chosen[0] == block
        for index in chosen[1:]:
            hit = hit | (index == block)
        used.append(hit.astype(jnp.int32))
    ahead = jnp.int32(0)
    behind = sum(used)
    for block in range(blocks):
        place = jnp.where(used[block] == 1, ahead, behind)
        ahead = ahead + used[block]
        behind = behind + 1 - used[block]
        plan[place] = jnp.int32(block)
        plan[blocks + block] = place
    for i in range(partners):
        plan[2 * blocks + i] = plan[blocks + chosen[i]]
    copies[2].wait()
    for k in range(number):
        code = pairs[1, 0, k]
        local = plan[blocks + pairs[2, 0, k]]
        plan[2 * blocks + partners + k] = jnp.where(code == 0, local, blocks + code - 1)
        plan[2 * blocks + partners + number + k] = plan[blocks + pairs[0, 0, k]]
    copies[1].wait()
    for index, out in zip(chosen, outs):
        out[...] = near[aligned(index, rows), :]
    for i in range(partners):
        front[span(i, rows), :] = near[aligned(plan[i], rows), :]
    for i in range(partners, blocks):
        back[span(i - partners, rows), :] = near[aligned(plan[i], rows), :]


def project(front, back, w_sent, w_received, sent, received):
    rows = front.shape[0]
    for side, nodes in ((pl.ds(0, rows), front), (pl.ds(rows, back.shape[0]), back)):
        sent[side, :] = product(nodes[...], w_sent[...]).astype(bf16)
        received[side, :] = product(nodes[...], w_received[...]).astype(bf16)


def load_kernel(
    front,
    back,
    edges,
    first,
    senders,
    receivers,
    edges_one,
    edges_two,
    w_edge,
    w_sent,
    w_received,
    base_one,
    base_two,
    sent,
    received,
    ends,
    flipped,
    near_senders,
    near_receivers,
    sems,
):
    rows = senders.shape[1]
    width = front.shape[1]
    half = edges_one.shape[0]
    copies = started(
        [
            (first.at[span(1, width), :], w_sent),
            (first.at[span(2, width), :], w_received),
            (first.at[span(0, width), :], w_edge),
            (edges.at[span(0, half), :], edges_one),
            (edges.at[span(1, half), :], edges_two),
            (senders, near_senders),
            (receivers, near_receivers),
        ],
        sems,
    )
    finish(copies[:2])
    project(front, back, w_sent, w_received, sent, received)
    finish(copies[2:4])
    base_one[...] = product(edges_one[...], w_edge[...])
    copies[4].wait()
    base_two[...] = product(edges_two[...], w_edge[...])
    finish(copies[5:])
    for block in range(senders.shape[0] // rows):
        here = span(block, rows)
        for side, source in enumerate((near_senders, near_receivers)):
            part = source[here, :].astype(f32)
            ends[here, side * rows : (side + 1) * rows] = part.astype(bf16)
            flipped[span(2 * block + side, rows), :] = part.T.astype(bf16)


def project_kernel(
    front, back, edges_one, w_edge, w_sent, w_received, base_one, sent, received
):
    project(front, back, w_sent, w_received, sent, received)
    base_one[...] = product(edges_one[...], w_edge[...])


def base_kernel(edges, w_edge, base):
    base[...] = product(edges[...], w_edge[...])


def edge_kernel(plan, flag, entering, *refs):
    edge_part(plan, refs[:-1])
    new_edges = refs[partners + 11 : partners + 13]
    half = new_edges[0].shape[0]

    @pl.when(flag[0] == 1)
    def _():
        finish(
            started([(entering.at[span(i, half), :], new_edges[i]) for i in range(2)], refs[-1])
        )


def edge_last_kernel(plan, *refs):
    edge_part(plan, refs)


def edge_part(plan, refs):
    incoming, refs = refs[:partners], refs[partners:]
    base = refs[0:2]
    sent, received, ends, flipped = refs[2:6]
    edges = refs[6:8]
    w_sent, second, gain = refs[8:11]
    new_edges = refs[11:13]
    low, sums = refs[13:15]
    outs = refs[15 : 15 + partners]
    (lookup,) = refs[15 + partners :]
    rows = incoming[0].shape[0]
    blocks = sent.shape[0] // rows
    half = edges[0].shape[0]
    number = 2 * half // rows
    sources = 2 * blocks + partners
    lookup[: blocks * rows, :] = sent[...]
    for i, block in enumerate(incoming):
        lookup[span(blocks + i, rows), :] = product(block[...], w_sent[...]).astype(bf16)
    sums[...] = jnp.zeros_like(sums)
    each = half // rows
    step = group if each % group == 0 else 1
    for start in range(0, number, step):
        part, begin = divmod(start, each)
        hidden = []
        for block in range(start, start + step):
            both = jnp.concatenate(
                [
                    lookup[aligned(plan[sources + block], rows), :],
                    received[aligned(plan[sources + number + block], rows), :],
                ],
                axis=0,
            )
            summed = base[part][span(block - part * each, rows), :] + product(
                ends[span(block, rows), :], both
            )
            hidden.append(jnp.maximum(summed, 0.0).astype(bf16))
        message = layer_norm(product(jnp.concatenate(hidden, axis=0), second[...]), gain[...])
        here = pl.ds(begin * rows, step * rows)
        new_edges[part][here, :] = (edges[part][here, :].astype(f32) + message).astype(bf16)
        rounded = message.astype(bf16)
        low[pl.ds(start * rows, step * rows), :] = rounded
        for i in range(step):
            block = start + i
            spread = product(
                flipped[span(2 * block, rows), :], rounded[i * rows : (i + 1) * rows, :]
            )
            sums[aligned(plan[sources + block], rows), :] += spread
    for i, out in enumerate(outs):
        out[...] = sums[span(blocks + i, rows), :].astype(bf16)


def node_update(nodes, ready, total, w_summed, second, gain):
    hidden = jnp.maximum(ready + product(total.astype(bf16), w_summed), 0.0).astype(bf16)
    update = layer_norm(product(hidden, second[...]), gain[...])
    return (nodes[...].astype(f32) + update).astype(bf16)


def settle(plan, low, flipped, sums, front, back, first, second, gain, own, ready, total):
    rows = flipped.shape[1]
    width = front.shape[1]
    blocks = (front.shape[0] + back.shape[0]) // rows
    number = low.shape[0] // rows
    targets = 2 * blocks + partners + number
    total[...] = sums[: blocks * rows, :]
    for block in range(number):
        spread = product(flipped[span(2 * block + 1, rows), :], low[span(block, rows), :])
        total[aligned(plan[targets + block], rows), :] += spread
    kept = partners * rows
    own[...] = total[:kept, :]
    ready[...] = product(front[...], first[:width, :])
    return node_update(
        back,
        product(back[...], first[:width, :]),
        total[kept:, :],
        first[width:, :],
        second,
        gain,
    )


def settle_kernel(
    plan, flag, low, flipped, sums, front, back, first, second, gain, entering, own, ready,
    new_back, total, sems,
):
    rows = flipped.shape[1]
    blocks = (front.shape[0] + back.shape[0]) // rows
    new_back[...] = settle(
        plan, low, flipped, sums, front, back, first, second, gain, own, ready, total
    )

    @pl.when(flag[0] == 1)
    def _():
        finish(
            started(
                [
                    (
                        entering.at[aligned(plan[partners + i], rows), :],
                        new_back.at[span(i, rows), :],
                    )
                    for i in range(blocks - partners)
                ],
                sems,
            )
        )


def settle_last_kernel(
    plan, low, flipped, sums, front, back, first, second, gain, edges_one, edges_two, own, ready,
    final_nodes, final_edges, total, near, sems,
):
    rows = flipped.shape[1]
    half = edges_one.shape[0]
    blocks = (front.shape[0] + back.shape[0]) // rows
    copies = started(
        [
            (edges_one, final_edges.at[span(0, half), :]),
            (edges_two, final_edges.at[span(1, half), :]),
        ],
        sems,
    )
    near[...] = settle(
        plan, low, flipped, sums, front, back, first, second, gain, own, ready, total
    )
    copies += started(
        [
            (near.at[span(i, rows), :], final_nodes.at[aligned(plan[partners + i], rows), :])
            for i in range(blocks - partners)
        ],
        sems,
        2,
    )
    finish(copies)


def node_part(plan, returned, own, ready, front, first, second, gain, total, blocks):
    rows = returned[0].shape[0]
    total[...] = own[...]
    for i, block in enumerate(returned):
        total[aligned(plan[2 * blocks + i], rows), :] += block[...].astype(f32)
    width = front.shape[1]
    return node_update(front, ready[...], total[...], first[width:, :], second, gain)


def node_kernel(plan, flag, *refs):
    returned, refs = refs[:partners], refs[partners:]
    own, ready, front, first, second, gain, entering, new_front, total, sems = refs
    rows = returned[0].shape[0]
    blocks = entering.shape[0] // rows
    new_front[...] = node_part(
        plan, returned, own, ready, front, first, second, gain, total, blocks
    )

    @pl.when(flag[0] == 1)
    def _():
        finish(
            started(
                [
                    (entering.at[aligned(plan[i], rows), :], new_front.at[span(i, rows), :])
                    for i in range(partners)
                ],
                sems,
            )
        )


def node_last_kernel(plan, *refs):
    returned, refs = refs[:partners], refs[partners:]
    own, ready, front, first, second, gain, _, final_nodes, total, near, sems = refs
    rows = returned[0].shape[0]
    blocks = final_nodes.shape[0] // rows
    near[...] = node_part(plan, returned, own, ready, front, first, second, gain, total, blocks)
    finish(
        started(
            [
                (near.at[span(i, rows), :], final_nodes.at[aligned(plan[i], rows), :])
                for i in range(partners)
            ],
            sems,
        )
    )


def ticks(
    node_latents,
    edge_latents,
    entering_nodes,
    entering_edges,
    edge_first,
    edge_second,
    edge_gain,
    node_first,
    node_second,
    node_gain,
    pair_list,
    send_list,
    senders,
    receivers,
):
    edge_second, node_first, node_second = edge_second[0], node_first[0], node_second[0]
    last = lax.axis_index("section") == lax.axis_size("section") - 1
    flag = last.astype(jnp.int32).reshape(1)
    node_rows, width = entering_nodes.shape
    edge_rows = entering_edges.shape[0]
    rows = senders.shape[1]
    blocks = node_rows // rows
    number = edge_rows // rows
    half = edge_rows // 2
    kept, rest = partners * rows, node_rows - partners * rows
    square = 2 * width * width
    block = ("v", shape((rows, width), bf16))
    front_out = ("v", shape((kept, width), bf16))
    back_out = ("v", shape((rest, width), bf16))
    half_low = ("v", shape((half, width), bf16))
    half_wide = ("v", shape((half, width), f32))
    weight = ("v", shape((width, width), bf16))
    all_low = ("v", shape((node_rows, width), bf16))
    slots = ("v", shape((node_rows + kept, width), f32))
    front_wide = ("v", shape((kept, width), f32))

    plan, front, back, *picked = call(
        plan_kernel,
        [("h", send_list), ("h", jnp.transpose(pair_list, (2, 0, 1))), ("h", node_latents[0])],
        [("s", shape((2 * blocks + partners + 2 * number,), jnp.int32)), front_out, back_out]
        + [block] * partners,
        scratch=[pltpu.VMEM((node_rows, width), bf16), pltpu.SMEM((1, partners), jnp.int32), pltpu.SMEM((3, 1, number), jnp.int32)],
        copies=3,
        moved=1 << 20,
    )

    def fetched(picked):
        return [rotated(picked[i], "dom", partner_offsets[i]) for i in range(partners)]

    def edge_stage(kernel, extra, incoming, base, sent, received, edges):
        new_one, new_two, low, sums, *partials = call(
            kernel,
            [("s", plan)]
            + extra
            + [("v", value) for value in (*incoming, *base, sent, received, ends, flipped)]
            + [("v", value) for value in (*edges, w_sent, edge_second, edge_gain)],
            [half_low, half_low, ("v", shape((edge_rows, width), bf16)), slots]
            + [block] * partners,
            scratch=[pltpu.VMEM((node_rows + kept, width), bf16)],
            copies=2 if extra else 0,
            flops=square * 2 * edge_rows,
            moved=16 << 20,
        )
        return (new_one, new_two), low, sums, partials

    def handed_back(partials):
        return [rotated(partials[i], "dom", -partner_offsets[i]) for i in range(partners)]

    incoming = fetched(picked)
    (
        edges_one,
        edges_two,
        w_edge,
        w_sent,
        w_received,
        base_one,
        base_two,
        sent,
        received,
        ends,
        flipped,
    ) = call(
        load_kernel,
        [("v", front), ("v", back)]
        + [("h", value) for value in (edge_latents[0], edge_first[0], senders, receivers)],
        [half_low, half_low, weight, weight, weight, half_wide, half_wide]
        + [all_low, all_low]
        + [("v", shape((edge_rows, 2 * rows), bf16)), ("v", shape((2 * edge_rows, rows), bf16))],
        scratch=[pltpu.VMEM((edge_rows, rows), jnp.int32)] * 2,
        copies=7,
        flops=square * (edge_rows + 2 * node_rows),
        moved=16 << 20,
    )
    edges, low, sums, partials = edge_stage(
        edge_kernel,
        [("s", flag), ("h", entering_edges)],
        incoming,
        (base_one, base_two), sent, received, (edges_one, edges_two)
    )
    edges_one = rotated(edges[0], "section", 1)
    returned = handed_back(partials)
    own, ready, new_back = call(
        settle_kernel,
        [("s", plan), ("s", flag)]
        + [
            ("v", value)
            for value in (low, flipped, sums, front, back, node_first, node_second, node_gain)
        ]
        + [("h", entering_nodes)],
        [front_wide, front_wide, back_out],
        scratch=[pltpu.VMEM((node_rows, width), f32)],
        copies=blocks - partners,
        flops=square * 2 * node_rows,
        moved=12 << 20,
    )
    back = rotated(new_back, "section", 1)
    (new_front,) = call(
        node_kernel,
        [("s", plan), ("s", flag)]
        + [
            ("v", value)
            for value in (*returned, own, ready, front, node_first, node_second, node_gain)
        ]
        + [("h", entering_nodes)],
        [front_out],
        scratch=[pltpu.VMEM((kept, width), f32)],
        copies=partners,
        flops=square * 2 * kept,
        moved=6 << 20,
    )
    front = rotated(new_front, "section", 1)
    edges_two = rotated(edges[1], "section", 1)

    picked = call(
        lambda plan, nodes, *outs: pick(plan, nodes, outs, blocks),
        [("s", plan), ("v", front)],
        [block] * partners,
        moved=1 << 20,
    )
    incoming = fetched(picked)
    base_one, sent, received = call(
        project_kernel,
        [("v", value) for value in (front, back, edges_one, w_edge, w_sent, w_received)],
        [half_wide, all_low, all_low],
        flops=square * (half + 2 * node_rows),
        moved=8 << 20,
    )
    (base_two,) = call(
        base_kernel,
        [("v", edges_two), ("v", w_edge)],
        [half_wide],
        flops=square * half,
        moved=3 << 20,
    )
    edges, low, sums, partials = edge_stage(
        edge_last_kernel,
        [],
        incoming,
        (base_one, base_two), sent, received, (edges_one, edges_two)
    )
    returned = handed_back(partials)
    own, ready, final_nodes, final_edges = call(
        settle_last_kernel,
        [("s", plan)]
        + [
            ("v", value)
            for value in (low, flipped, sums, front, back, node_first, node_second, node_gain)
        ]
        + [("v", value) for value in edges],
        [front_wide, front_wide]
        + [("h", shape((node_rows, width), bf16)), ("h", shape((edge_rows, width), bf16))],
        scratch=[pltpu.VMEM((node_rows, width), f32), pltpu.VMEM((rest, width), bf16)],
        copies=2 + blocks - partners,
        flops=square * 2 * node_rows,
        moved=12 << 20,
    )
    (final_nodes,) = call(
        node_last_kernel,
        [("s", plan)]
        + [
            ("v", value)
            for value in (*returned, own, ready, front, node_first, node_second, node_gain)
        ]
        + [("h", final_nodes)],
        [("h", shape((node_rows, width), bf16))],
        scratch=[pltpu.VMEM((kept, width), f32), pltpu.VMEM((kept, width), bf16)],
        copies=partners,
        aliases={7 + partners: 0},
        flops=square * 2 * kept,
        moved=6 << 20,
    )
    return (final_nodes[None], final_edges[None])


def pick(plan, nodes, outs, blocks):
    rows = outs[0].shape[0]
    for i, out in enumerate(outs):
        out[...] = nodes[aligned(plan[2 * blocks + i], rows), :]


def solution(mesh):
    placed = (
        P("section", "dom", None),
        P("section", "dom", None),
        P("dom", None),
        P("dom", None),
        P("section", None, None),
        P("section", None, None),
        P("section", None),
        P("section", None, None),
        P("section", None, None),
        P("section", None),
        P("dom", None, None),
        P("dom", None),
        P("dom", None),
        P("dom", None),
    )
    return jax.shard_map(
        ticks,
        mesh=mesh,
        in_specs=placed,
        out_specs=(P("section", "dom", None), P("section", "dom", None)),
        check_vma=False,
    )
```

```python
import jax
import jax.numpy as jnp
from jax import lax
from jax.experimental import pallas as pl
from jax.experimental.pallas import tpu as pltpu
from jax.sharding import PartitionSpec as P


exchanges = ((1, 1), (2, 0), (2, 1), (1, 0))
partners = len(exchanges)
epsilon = 1e-05
f32 = jnp.float32
bf16 = jnp.bfloat16
VMEM = pl.BlockSpec(memory_space=pltpu.VMEM)
SMEM = pl.BlockSpec(memory_space=pltpu.SMEM)
HBM = pl.BlockSpec(memory_space=pltpu.HBM)
group = 3


def passed_along(block, axis, distance):
    count = lax.axis_size(axis)
    return lax.ppermute(block, axis, [(i, (i + distance) % count) for i in range(count)])


def swapped(block, step, phase):
    count = lax.axis_size("dom")
    assert count % (2 * step) == 0
    route = [
        (i, (i + (step if (i // step) % 2 == phase else -step)) % count) for i in range(count)
    ]
    return lax.ppermute(block, "dom", route)


def layer_norm(values, gain):
    centred = values - jnp.mean(values, axis=-1, keepdims=True)
    spread = jnp.mean(centred * centred, axis=-1, keepdims=True)
    return centred * lax.rsqrt(spread + epsilon) * gain


def product(left, right):
    return jnp.dot(left, right, preferred_element_type=f32)


def shape(dims, kind):
    return jax.ShapeDtypeStruct(dims, kind)


def call(kernel, ins, outs, scratch=(), copies=0, aliases=None, flops=0, moved=0):
    specs = {"v": VMEM, "s": SMEM, "h": HBM}
    scratch = list(scratch)
    if copies:
        scratch.append(pltpu.SemaphoreType.DMA((copies,)))
    step = pl.pallas_call(
        kernel,
        out_shape=tuple(out for _, out in outs),
        in_specs=[specs[place] for place, _ in ins],
        out_specs=tuple(specs[place] for place, _ in outs),
        scratch_shapes=scratch,
        input_output_aliases=aliases or {},
        compiler_params=pltpu.CompilerParams(vmem_limit_bytes=24 << 20),
        cost_estimate=pl.CostEstimate(flops=flops, bytes_accessed=moved, transcendentals=0),
    )
    values = [
            pltpu.with_memory_space_constraint(value, pltpu.HBM) if place == "h" else value
            for place, value in ins
    ]
    return step(*values)


def started(pairs, sems, first=0):
    copies = [
        pltpu.make_async_copy(source, target, sems.at[first + i])
        for i, (source, target) in enumerate(pairs)
    ]
    for copy in copies:
        copy.start()
    return copies


def finish(copies):
    for copy in copies:
        copy.wait()


def aligned(index, rows):
    return pl.ds(pl.multiple_of(index * rows, rows), rows)


def halves(whole, one):
    rows = one.shape[0]
    return whole.at[pl.ds(0, rows), :], whole.at[pl.ds(rows, whole.shape[0] - rows), :]


def span(index, rows):
    return pl.ds(index * rows, rows)


def plan_kernel(place_here, sends_far, pairs_far, nodes, plan, front, back, *rest):
    outs, (near, sends, pairs, sems) = rest[:partners], rest[partners:]
    rows = outs[0].shape[0]
    blocks = nodes.shape[0] // rows
    number = pairs.shape[2]
    copies = started([(sends_far, sends), (nodes, near), (pairs_far, pairs)], sems)
    copies[0].wait()
    chosen, ahead_of = [], []
    for step, phase in exchanges:
        ahead_of.append(lax.rem(place_here[0] // step, 2) == phase)
        slot = 2 * (step - 1)
        chosen.append(jnp.where(ahead_of[-1], sends[0, slot], sends[0, slot + 1]))
    used = []
    for block in range(blocks):
        hit = chosen[0] == block
        for index in chosen[1:]:
            hit = hit | (index == block)
        used.append(hit.astype(jnp.int32))
    ahead = jnp.int32(0)
    behind = sum(used)
    for block in range(blocks):
        place = jnp.where(used[block] == 1, ahead, behind)
        ahead = ahead + used[block]
        behind = behind + 1 - used[block]
        plan[place] = jnp.int32(block)
        plan[blocks + block] = place
    for i in range(partners):
        plan[2 * blocks + i] = plan[blocks + chosen[i]]
    copies[2].wait()
    for k in range(number):
        code = pairs[1, 0, k]
        local = plan[blocks + pairs[2, 0, k]]
        source = local
        for i, (step, _) in enumerate(exchanges):
            arrives = 2 * (step - 1) + 1 + ahead_of[i].astype(jnp.int32)
            source = jnp.where(code == arrives, blocks + i, source)
        plan[2 * blocks + partners + k] = source
        plan[2 * blocks + partners + number + k] = plan[blocks + pairs[0, 0, k]]
    copies[1].wait()
    for index, out in zip(chosen, outs):
        out[...] = near[aligned(index, rows), :]
    for i in range(partners):
        front[span(i, rows), :] = near[aligned(plan[i], rows), :]
    for i in range(partners, blocks):
        back[span(i - partners, rows), :] = near[aligned(plan[i], rows), :]


def project(front, back, w_sent, w_received, sent, received):
    rows = front.shape[0]
    for side, nodes in ((pl.ds(0, rows), front), (pl.ds(rows, back.shape[0]), back)):
        sent[side, :] = product(nodes[...], w_sent[...]).astype(bf16)
        received[side, :] = product(nodes[...], w_received[...]).astype(bf16)


def load_kernel(
    front,
    back,
    edges,
    first,
    senders,
    receivers,
    edges_one,
    edges_two,
    w_edge,
    w_sent,
    w_received,
    base_one,
    base_two,
    sent,
    received,
    ends,
    flipped,
    near_senders,
    near_receivers,
    sems,
):
    rows = senders.shape[1]
    width = front.shape[1]
    near_one, near_two = halves(edges, edges_one)
    copies = started(
        [
            (first.at[span(1, width), :], w_sent),
            (first.at[span(2, width), :], w_received),
            (first.at[span(0, width), :], w_edge),
            (near_one, edges_one),
            (near_two, edges_two),
            (senders, near_senders),
            (receivers, near_receivers),
        ],
        sems,
    )
    finish(copies[:2])
    project(front, back, w_sent, w_received, sent, received)
    finish(copies[2:4])
    base_one[...] = product(edges_one[...], w_edge[...])
    copies[4].wait()
    base_two[...] = product(edges_two[...], w_edge[...])
    finish(copies[5:])
    for block in range(senders.shape[0] // rows):
        here = span(block, rows)
        for side, source in enumerate((near_senders, near_receivers)):
            part = source[here, :].astype(f32)
            ends[here, side * rows : (side + 1) * rows] = part.astype(bf16)
            flipped[span(2 * block + side, rows), :] = part.T.astype(bf16)


def project_kernel(
    front, back, edges_one, w_edge, w_sent, w_received, base_one, sent, received
):
    project(front, back, w_sent, w_received, sent, received)
    base_one[...] = product(edges_one[...], w_edge[...])


def base_kernel(edges, w_edge, base):
    base[...] = product(edges[...], w_edge[...])


def edge_kernel(plan, flag, entering, *refs):
    edge_part(plan, refs[:-1])
    one, two = refs[partners + 11 : partners + 13]

    @pl.when(flag[0] == 1)
    def _():
        finish(started(zip(halves(entering, one), (one, two)), refs[-1]))


def edge_last_kernel(plan, *refs):
    edge_part(plan, refs)


def edge_part(plan, refs):
    incoming, refs = refs[:partners], refs[partners:]
    base = refs[0:2]
    sent, received, ends, flipped = refs[2:6]
    edges = refs[6:8]
    w_sent, second, gain = refs[8:11]
    new_edges = refs[11:13]
    low, sums = refs[13:15]
    outs = refs[15 : 15 + partners]
    (lookup,) = refs[15 + partners :]
    rows = incoming[0].shape[0]
    blocks = sent.shape[0] // rows
    number = low.shape[0] // rows
    each = edges[0].shape[0] // rows
    sources = 2 * blocks + partners
    lookup[: blocks * rows, :] = sent[...]
    for i, block in enumerate(incoming):
        lookup[span(blocks + i, rows), :] = product(block[...], w_sent[...]).astype(bf16)
    sums[...] = jnp.zeros_like(sums)
    step = group if each % group == 0 and number % group == 0 else 1
    starts = list(range(0, number, step))

    def opened(start):
        part = int(start >= each)
        hidden = []
        for block in range(start, start + step):
            both = jnp.concatenate(
                [
                    lookup[aligned(plan[sources + block], rows), :],
                    received[aligned(plan[sources + number + block], rows), :],
                ],
                axis=0,
            )
            summed = base[part][span(block - part * each, rows), :] + product(
                ends[span(block, rows), :], both
            )
            hidden.append(jnp.maximum(summed, 0.0).astype(bf16))
        return product(jnp.concatenate(hidden, axis=0), second[...])

    def closed(start, raw):
        part = int(start >= each)
        begin = start - part * each
        message = layer_norm(raw, gain[...])
        here = pl.ds(begin * rows, step * rows)
        new_edges[part][here, :] = (edges[part][here, :].astype(f32) + message).astype(bf16)
        rounded = message.astype(bf16)
        low[pl.ds(start * rows, step * rows), :] = rounded
        for i in range(step):
            block = start + i
            spread = product(
                flipped[span(2 * block, rows), :], rounded[i * rows : (i + 1) * rows, :]
            )
            sums[aligned(plan[sources + block], rows), :] += spread

    raw = opened(starts[0])
    for now, later in zip(starts, starts[1:] + [None]):
        ahead = None if later is None else opened(later)
        closed(now, raw)
        raw = ahead
    for i, out in enumerate(outs):
        out[...] = sums[span(blocks + i, rows), :].astype(bf16)


def node_update(nodes, ready, total, w_summed, second, gain):
    hidden = jnp.maximum(ready + product(total.astype(bf16), w_summed), 0.0).astype(bf16)
    update = layer_norm(product(hidden, second[...]), gain[...])
    return (nodes[...].astype(f32) + update).astype(bf16)


def settle(plan, low, flipped, sums, front, back, first, second, gain, own, ready, total):
    rows = flipped.shape[1]
    width = front.shape[1]
    blocks = (front.shape[0] + back.shape[0]) // rows
    number = low.shape[0] // rows
    targets = 2 * blocks + partners + number
    total[...] = sums[: blocks * rows, :]
    for block in range(number):
        spread = product(flipped[span(2 * block + 1, rows), :], low[span(block, rows), :])
        total[aligned(plan[targets + block], rows), :] += spread
    kept = partners * rows
    own[...] = total[:kept, :]
    ready[...] = product(front[...], first[:width, :])
    return node_update(
        back,
        product(back[...], first[:width, :]),
        total[kept:, :],
        first[width:, :],
        second,
        gain,
    )


def settle_kernel(
    plan, flag, low, flipped, sums, front, back, first, second, gain, entering, own, ready,
    new_back, total, sems,
):
    rows = flipped.shape[1]
    blocks = (front.shape[0] + back.shape[0]) // rows
    new_back[...] = settle(
        plan, low, flipped, sums, front, back, first, second, gain, own, ready, total
    )

    @pl.when(flag[0] == 1)
    def _():
        finish(
            started(
                [
                    (
                        entering.at[aligned(plan[partners + i], rows), :],
                        new_back.at[span(i, rows), :],
                    )
                    for i in range(blocks - partners)
                ],
                sems,
            )
        )


def settle_last_kernel(
    plan, low, flipped, sums, front, back, first, second, gain, edges_one, edges_two, own, ready,
    final_nodes, final_edges, total, near, sems,
):
    rows = flipped.shape[1]
    far_one, far_two = halves(final_edges, edges_one)
    blocks = (front.shape[0] + back.shape[0]) // rows
    copies = started([(edges_one, far_one), (edges_two, far_two)], sems)
    near[...] = settle(
        plan, low, flipped, sums, front, back, first, second, gain, own, ready, total
    )
    copies += started(
        [
            (near.at[span(i, rows), :], final_nodes.at[aligned(plan[partners + i], rows), :])
            for i in range(blocks - partners)
        ],
        sems,
        2,
    )
    finish(copies)


def node_part(plan, returned, own, ready, front, first, second, gain, total, blocks):
    rows = returned[0].shape[0]
    total[...] = own[...]
    for i, block in enumerate(returned):
        total[aligned(plan[2 * blocks + i], rows), :] += block[...].astype(f32)
    width = front.shape[1]
    return node_update(front, ready[...], total[...], first[width:, :], second, gain)


def node_kernel(plan, flag, *refs):
    returned, refs = refs[:partners], refs[partners:]
    own, ready, front, first, second, gain, entering, new_front, total, sems = refs
    rows = returned[0].shape[0]
    blocks = entering.shape[0] // rows
    new_front[...] = node_part(
        plan, returned, own, ready, front, first, second, gain, total, blocks
    )

    @pl.when(flag[0] == 1)
    def _():
        finish(
            started(
                [
                    (entering.at[aligned(plan[i], rows), :], new_front.at[span(i, rows), :])
                    for i in range(partners)
                ],
                sems,
            )
        )


def node_last_kernel(plan, *refs):
    returned, refs = refs[:partners], refs[partners:]
    own, ready, front, first, second, gain, _, final_nodes, total, near, sems = refs
    rows = returned[0].shape[0]
    blocks = final_nodes.shape[0] // rows
    near[...] = node_part(plan, returned, own, ready, front, first, second, gain, total, blocks)
    finish(
        started(
            [
                (near.at[span(i, rows), :], final_nodes.at[aligned(plan[i], rows), :])
                for i in range(partners)
            ],
            sems,
        )
    )


def ticks(
    node_latents,
    edge_latents,
    entering_nodes,
    entering_edges,
    edge_first,
    edge_second,
    edge_gain,
    node_first,
    node_second,
    node_gain,
    pair_list,
    send_list,
    senders,
    receivers,
):
    edge_second, node_first, node_second = edge_second[0], node_first[0], node_second[0]
    last = lax.axis_index("section") == lax.axis_size("section") - 1
    flag = last.astype(jnp.int32).reshape(1)
    here = lax.axis_index("dom").astype(jnp.int32).reshape(1)
    node_rows, width = entering_nodes.shape
    edge_rows = entering_edges.shape[0]
    rows = senders.shape[1]
    blocks = node_rows // rows
    number = edge_rows // rows
    one_rows = number // 2 * rows
    two_rows = edge_rows - one_rows
    kept, rest = partners * rows, node_rows - partners * rows
    square = 2 * width * width
    block = ("v", shape((rows, width), bf16))
    front_out = ("v", shape((kept, width), bf16))
    back_out = ("v", shape((rest, width), bf16))
    one_low = ("v", shape((one_rows, width), bf16))
    two_low = ("v", shape((two_rows, width), bf16))
    one_wide = ("v", shape((one_rows, width), f32))
    two_wide = ("v", shape((two_rows, width), f32))
    weight = ("v", shape((width, width), bf16))
    all_low = ("v", shape((node_rows, width), bf16))
    slots = ("v", shape((node_rows + kept, width), f32))
    front_wide = ("v", shape((kept, width), f32))

    plan, front, back, *picked = call(
        plan_kernel,
        [("s", here), ("h", send_list), ("h", jnp.transpose(pair_list, (2, 0, 1))), ("h", node_latents[0])],
        [("s", shape((2 * blocks + partners + 2 * number,), jnp.int32)), front_out, back_out]
        + [block] * partners,
        scratch=[pltpu.VMEM((node_rows, width), bf16), pltpu.SMEM((1, partners), jnp.int32), pltpu.SMEM((3, 1, number), jnp.int32)],
        copies=3,
        moved=1 << 20,
    )

    def fetched(picked):
        return [swapped(picked[i], *exchanges[i]) for i in range(partners)]

    def edge_stage(kernel, extra, incoming, base, sent, received, edges):
        new_one, new_two, low, sums, *partials = call(
            kernel,
            [("s", plan)]
            + extra
            + [("v", value) for value in (*incoming, *base, sent, received, ends, flipped)]
            + [("v", value) for value in (*edges, w_sent, edge_second, edge_gain)],
            [one_low, two_low, ("v", shape((edge_rows, width), bf16)), slots]
            + [block] * partners,
            scratch=[pltpu.VMEM((node_rows + kept, width), bf16)],
            copies=2 if extra else 0,
            flops=square * 2 * edge_rows,
            moved=16 << 20,
        )
        return (new_one, new_two), low, sums, partials

    def handed_back(partials):
        return [swapped(partials[i], *exchanges[i]) for i in range(partners)]

    incoming = fetched(picked)
    (
        edges_one,
        edges_two,
        w_edge,
        w_sent,
        w_received,
        base_one,
        base_two,
        sent,
        received,
        ends,
        flipped,
    ) = call(
        load_kernel,
        [("v", front), ("v", back)]
        + [("h", value) for value in (edge_latents[0], edge_first[0], senders, receivers)],
        [one_low, two_low, weight, weight, weight, one_wide, two_wide]
        + [all_low, all_low]
        + [("v", shape((edge_rows, 2 * rows), bf16)), ("v", shape((2 * edge_rows, rows), bf16))],
        scratch=[pltpu.VMEM((edge_rows, rows), jnp.int32)] * 2,
        copies=7,
        flops=square * (edge_rows + 2 * node_rows),
        moved=16 << 20,
    )
    edges, low, sums, partials = edge_stage(
        edge_kernel,
        [("s", flag), ("h", entering_edges)],
        incoming,
        (base_one, base_two), sent, received, (edges_one, edges_two)
    )
    edges_one = passed_along(edges[0], "section", 1)
    returned = handed_back(partials)
    own, ready, new_back = call(
        settle_kernel,
        [("s", plan), ("s", flag)]
        + [
            ("v", value)
            for value in (low, flipped, sums, front, back, node_first, node_second, node_gain)
        ]
        + [("h", entering_nodes)],
        [front_wide, front_wide, back_out],
        scratch=[pltpu.VMEM((node_rows, width), f32)],
        copies=blocks - partners,
        flops=square * 2 * node_rows,
        moved=12 << 20,
    )
    back = passed_along(new_back, "section", 1)
    (new_front,) = call(
        node_kernel,
        [("s", plan), ("s", flag)]
        + [
            ("v", value)
            for value in (*returned, own, ready, front, node_first, node_second, node_gain)
        ]
        + [("h", entering_nodes)],
        [front_out],
        scratch=[pltpu.VMEM((kept, width), f32)],
        copies=partners,
        flops=square * 2 * kept,
        moved=6 << 20,
    )
    front = passed_along(new_front, "section", 1)
    edges_two = passed_along(edges[1], "section", 1)

    picked = call(
        lambda plan, nodes, *outs: pick(plan, nodes, outs, blocks),
        [("s", plan), ("v", front)],
        [block] * partners,
        moved=1 << 20,
    )
    incoming = fetched(picked)
    base_one, sent, received = call(
        project_kernel,
        [("v", value) for value in (front, back, edges_one, w_edge, w_sent, w_received)],
        [one_wide, all_low, all_low],
        flops=square * (one_rows + 2 * node_rows),
        moved=8 << 20,
    )
    (base_two,) = call(
        base_kernel,
        [("v", edges_two), ("v", w_edge)],
        [two_wide],
        flops=square * two_rows,
        moved=3 << 20,
    )
    edges, low, sums, partials = edge_stage(
        edge_last_kernel,
        [],
        incoming,
        (base_one, base_two), sent, received, (edges_one, edges_two)
    )
    returned = handed_back(partials)
    own, ready, final_nodes, final_edges = call(
        settle_last_kernel,
        [("s", plan)]
        + [
            ("v", value)
            for value in (low, flipped, sums, front, back, node_first, node_second, node_gain)
        ]
        + [("v", value) for value in edges],
        [front_wide, front_wide]
        + [("h", shape((node_rows, width), bf16)), ("h", shape((edge_rows, width), bf16))],
        scratch=[pltpu.VMEM((node_rows, width), f32), pltpu.VMEM((rest, width), bf16)],
        copies=2 + blocks - partners,
        flops=square * 2 * node_rows,
        moved=12 << 20,
    )
    (final_nodes,) = call(
        node_last_kernel,
        [("s", plan)]
        + [
            ("v", value)
            for value in (*returned, own, ready, front, node_first, node_second, node_gain)
        ]
        + [("h", final_nodes)],
        [("h", shape((node_rows, width), bf16))],
        scratch=[pltpu.VMEM((kept, width), f32), pltpu.VMEM((kept, width), bf16)],
        copies=partners,
        aliases={7 + partners: 0},
        flops=square * 2 * kept,
        moved=6 << 20,
    )
    return (final_nodes[None], final_edges[None])


def pick(plan, nodes, outs, blocks):
    rows = outs[0].shape[0]
    for i, out in enumerate(outs):
        out[...] = nodes[aligned(plan[2 * blocks + i], rows), :]


def solution(mesh):
    placed = (
        P("section", "dom", None),
        P("section", "dom", None),
        P("dom", None),
        P("dom", None),
        P("section", None, None),
        P("section", None, None),
        P("section", None),
        P("section", None, None),
        P("section", None, None),
        P("section", None),
        P("dom", None, None),
        P("dom", None),
        P("dom", None),
        P("dom", None),
    )
    return jax.shard_map(
        ticks,
        mesh=mesh,
        in_specs=placed,
        out_specs=(P("section", "dom", None), P("section", "dom", None)),
        check_vma=False,
    )
```

```python
import functools

import jax
import jax.numpy as jnp
from jax import lax
from jax.experimental import pallas as pl
from jax.experimental.pallas import tpu as pltpu
from jax.sharding import PartitionSpec as P


exchanges = ((1, 1), (2, 0), (2, 1), (1, 0))
partners = len(exchanges)
epsilon = 1e-05
f32 = jnp.float32
bf16 = jnp.bfloat16
VMEM = pl.BlockSpec(memory_space=pltpu.VMEM)
SMEM = pl.BlockSpec(memory_space=pltpu.SMEM)
HBM = pl.BlockSpec(memory_space=pltpu.HBM)
group = 3


def passed_along(block, axis, distance):
    count = lax.axis_size(axis)
    return lax.ppermute(block, axis, [(i, (i + distance) % count) for i in range(count)])


def swapped(block, step, phase):
    count = lax.axis_size("dom")
    assert count % (2 * step) == 0
    route = [
        (i, (i + (step if (i // step) % 2 == phase else -step)) % count) for i in range(count)
    ]
    return lax.ppermute(block, "dom", route)


def layer_norm(values, gain):
    centred = values - jnp.mean(values, axis=-1, keepdims=True)
    spread = jnp.mean(centred * centred, axis=-1, keepdims=True)
    return centred * lax.rsqrt(spread + epsilon) * gain


def product(left, right):
    return jnp.dot(left, right, preferred_element_type=f32)


def shape(dims, kind):
    return jax.ShapeDtypeStruct(dims, kind)


def call(kernel, ins, outs, scratch=(), copies=0, aliases=None, flops=0, moved=0):
    specs = {"v": VMEM, "s": SMEM, "h": HBM}
    scratch = list(scratch)
    if copies:
        scratch.append(pltpu.SemaphoreType.DMA((copies,)))
    step = pl.pallas_call(
        kernel,
        out_shape=tuple(out for _, out in outs),
        in_specs=[specs[place] for place, _ in ins],
        out_specs=tuple(specs[place] for place, _ in outs),
        scratch_shapes=scratch,
        input_output_aliases=aliases or {},
        compiler_params=pltpu.CompilerParams(vmem_limit_bytes=24 << 20),
        cost_estimate=pl.CostEstimate(flops=flops, bytes_accessed=moved, transcendentals=0),
    )
    values = [
            pltpu.with_memory_space_constraint(value, pltpu.HBM) if place == "h" else value
            for place, value in ins
    ]
    return step(*values)


def started(pairs, sems, first=0):
    copies = [
        pltpu.make_async_copy(source, target, sems.at[first + i])
        for i, (source, target) in enumerate(pairs)
    ]
    for copy in copies:
        copy.start()
    return copies


def finish(copies):
    for copy in copies:
        copy.wait()


def aligned(index, rows):
    return pl.ds(pl.multiple_of(index * rows, rows), rows)


def halves(whole, one):
    rows = one.shape[0]
    return whole.at[pl.ds(0, rows), :], whole.at[pl.ds(rows, whole.shape[0] - rows), :]


def span(index, rows):
    return pl.ds(index * rows, rows)


def plan_kernel(place_here, sends_far, pairs_far, nodes, plan, near, *rest):
    outs, (sends, pairs, sems) = rest[:partners], rest[partners:]
    rows = outs[0].shape[0]
    blocks = nodes.shape[0] // rows
    number = pairs.shape[2]
    copies = started([(sends_far, sends), (nodes, near), (pairs_far, pairs)], sems)
    copies[0].wait()
    chosen, ahead_of = [], []
    for step, phase in exchanges:
        ahead_of.append(lax.rem(place_here[0] // step, 2) == phase)
        slot = 2 * (step - 1)
        chosen.append(jnp.where(ahead_of[-1], sends[0, slot], sends[0, slot + 1]))
    ahead = jnp.int32(0)
    places = []
    for i, index in enumerate(chosen):
        place, new = ahead, jnp.int32(1)
        for earlier, where in zip(chosen[:i], places):
            place = jnp.where(earlier == index, where, place)
            new = jnp.where(earlier == index, 0, new)
        places.append(place)
        plan[place] = index
        plan[blocks + index] = place
        plan[2 * blocks + i] = place
        ahead = ahead + new
    for block in range(blocks):
        free = chosen[0] != block
        for index in chosen[1:]:
            free = free & (index != block)

        @pl.when(free)
        def _(block=block, ahead=ahead):
            plan[ahead] = jnp.int32(block)
            plan[blocks + block] = ahead

        ahead = ahead + free.astype(jnp.int32)
    finish(copies[1:])
    for index, out in zip(chosen, outs):
        out[...] = near[aligned(index, rows), :]
    for k in range(number):
        code = pairs[1, 0, k]
        local = plan[blocks + pairs[2, 0, k]]
        source = local
        for i, (step, _) in enumerate(exchanges):
            arrives = 2 * (step - 1) + 1 + ahead_of[i].astype(jnp.int32)
            source = jnp.where(code == arrives, blocks + i, source)
        plan[2 * blocks + partners + k] = source
        plan[2 * blocks + partners + number + k] = plan[blocks + pairs[0, 0, k]]


def project(front, back, w_sent, w_received, sent, received):
    rows = front.shape[0]
    for side, nodes in ((pl.ds(0, rows), front), (pl.ds(rows, back.shape[0]), back)):
        sent[side, :] = product(nodes[...], w_sent[...]).astype(bf16)
        received[side, :] = product(nodes[...], w_received[...]).astype(bf16)


def load_kernel(
    plan,
    nodes,
    edges,
    first,
    senders,
    receivers,
    front,
    back,
    edges_one,
    edges_two,
    w_edge,
    w_sent,
    w_received,
    base_one,
    base_two,
    sent,
    received,
    ends,
    flipped,
    near_senders,
    near_receivers,
    sems,
):
    rows = senders.shape[1]
    width = front.shape[1]
    near_one, near_two = halves(edges, edges_one)
    copies = started(
        [
            (first.at[span(1, width), :], w_sent),
            (first.at[span(2, width), :], w_received),
            (first.at[span(0, width), :], w_edge),
            (near_one, edges_one),
            (near_two, edges_two),
            (senders, near_senders),
            (receivers, near_receivers),
        ],
        sems,
    )
    kept = front.shape[0] // rows
    for i in range(kept):
        front[span(i, rows), :] = nodes[aligned(plan[i], rows), :]
    for i in range(back.shape[0] // rows):
        back[span(i, rows), :] = nodes[aligned(plan[kept + i], rows), :]
    finish(copies[:2])
    project(front, back, w_sent, w_received, sent, received)
    finish(copies[2:4])
    base_one[...] = product(edges_one[...], w_edge[...])
    copies[4].wait()
    base_two[...] = product(edges_two[...], w_edge[...])
    finish(copies[5:])
    for block in range(senders.shape[0] // rows):
        here = span(block, rows)
        for side, source in enumerate((near_senders, near_receivers)):
            part = source[here, :].astype(f32)
            ends[here, side * rows : (side + 1) * rows] = part.astype(bf16)
            flipped[span(2 * block + side, rows), :] = part.T.astype(bf16)


def pick_kernel(base, plan, nodes, *outs):
    pick(plan, nodes, outs, base)


def join_kernel(base, plan, one, two, front, *outs):
    half = one.shape[0]
    front[:half, :] = one[...]
    front[half:, :] = two[...]
    pick(plan, front, outs, base + partners - len(outs))


def pick(plan, nodes, outs, first):
    rows = outs[0].shape[0]
    for i, out in enumerate(outs):
        out[...] = nodes[aligned(plan[first + i], rows), :]


def project_kernel(
    front, back, edges_one, w_edge, w_sent, w_received, base_one, sent, received
):
    project(front, back, w_sent, w_received, sent, received)
    base_one[...] = product(edges_one[...], w_edge[...])


def base_kernel(edges, w_edge, base):
    base[...] = product(edges[...], w_edge[...])


def edge_kernel(plan, flag, entering, *refs):
    edge_part(plan, refs[:-1])
    one, two = refs[partners + 11 : partners + 13]

    @pl.when(flag[0] == 1)
    def _():
        finish(started(zip(halves(entering, one), (one, two)), refs[-1]))


def edge_last_kernel(plan, *refs):
    edge_part(plan, refs)


def edge_part(plan, refs):
    incoming, refs = refs[:partners], refs[partners:]
    base = refs[0:2]
    sent, received, ends, flipped = refs[2:6]
    edges = refs[6:8]
    w_sent, second, gain = refs[8:11]
    new_edges = refs[11:13]
    low, sums = refs[13:15]
    outs = refs[15 : 15 + partners]
    (lookup,) = refs[15 + partners :]
    rows = incoming[0].shape[0]
    blocks = sent.shape[0] // rows
    number = low.shape[0] // rows
    each = edges[0].shape[0] // rows
    sources = 2 * blocks + partners
    lookup[: blocks * rows, :] = sent[...]
    for i, block in enumerate(incoming):
        lookup[span(blocks + i, rows), :] = product(block[...], w_sent[...]).astype(bf16)
    sums[...] = jnp.zeros_like(sums)
    step = group if each % group == 0 and number % group == 0 else 1
    starts = list(range(0, number, step))

    def opened(start):
        part = int(start >= each)
        hidden = []
        for block in range(start, start + step):
            both = jnp.concatenate(
                [
                    lookup[aligned(plan[sources + block], rows), :],
                    received[aligned(plan[sources + number + block], rows), :],
                ],
                axis=0,
            )
            summed = base[part][span(block - part * each, rows), :] + product(
                ends[span(block, rows), :], both
            )
            hidden.append(jnp.maximum(summed, 0.0).astype(bf16))
        return product(jnp.concatenate(hidden, axis=0), second[...])

    def closed(start, raw):
        part = int(start >= each)
        begin = start - part * each
        message = layer_norm(raw, gain[...])
        here = pl.ds(begin * rows, step * rows)
        new_edges[part][here, :] = (edges[part][here, :].astype(f32) + message).astype(bf16)
        rounded = message.astype(bf16)
        low[pl.ds(start * rows, step * rows), :] = rounded
        for i in range(step):
            block = start + i
            spread = product(
                flipped[span(2 * block, rows), :], rounded[i * rows : (i + 1) * rows, :]
            )
            sums[aligned(plan[sources + block], rows), :] += spread

    raw = opened(starts[0])
    for now, later in zip(starts, starts[1:] + [None]):
        ahead = None if later is None else opened(later)
        closed(now, raw)
        raw = ahead
    for i, out in enumerate(outs):
        out[...] = sums[span(blocks + i, rows), :].astype(bf16)


def node_update(nodes, ready, total, w_summed, second, gain):
    hidden = jnp.maximum(ready + product(total.astype(bf16), w_summed), 0.0).astype(bf16)
    update = layer_norm(product(hidden, second[...]), gain[...])
    return (nodes[...].astype(f32) + update).astype(bf16)


def settle(plan, low, flipped, sums, front, back, first, second, gain, own, ready, total):
    rows = flipped.shape[1]
    width = front.shape[1]
    blocks = (front.shape[0] + back.shape[0]) // rows
    number = low.shape[0] // rows
    targets = 2 * blocks + partners + number
    total[...] = sums[: blocks * rows, :]
    for block in range(number):
        spread = product(flipped[span(2 * block + 1, rows), :], low[span(block, rows), :])
        total[aligned(plan[targets + block], rows), :] += spread
    kept = partners * rows
    own[...] = total[:kept, :]
    ready[...] = product(front[...], first[:width, :])
    return node_update(
        back,
        product(back[...], first[:width, :]),
        total[kept:, :],
        first[width:, :],
        second,
        gain,
    )


def settle_kernel(
    plan, flag, low, flipped, sums, front, back, first, second, gain, entering, own, ready,
    new_back, total, sems,
):
    rows = flipped.shape[1]
    blocks = (front.shape[0] + back.shape[0]) // rows
    new_back[...] = settle(
        plan, low, flipped, sums, front, back, first, second, gain, own, ready, total
    )

    @pl.when(flag[0] == 1)
    def _():
        finish(
            started(
                [
                    (
                        entering.at[aligned(plan[partners + i], rows), :],
                        new_back.at[span(i, rows), :],
                    )
                    for i in range(blocks - partners)
                ],
                sems,
            )
        )


def settle_last_kernel(
    plan, low, flipped, sums, front, back, first, second, gain, edges_one, edges_two, own, ready,
    final_nodes, final_edges, total, near, sems,
):
    rows = flipped.shape[1]
    far_one, far_two = halves(final_edges, edges_one)
    blocks = (front.shape[0] + back.shape[0]) // rows
    copies = started([(edges_one, far_one), (edges_two, far_two)], sems)
    near[...] = settle(
        plan, low, flipped, sums, front, back, first, second, gain, own, ready, total
    )
    copies += started(
        [
            (near.at[span(i, rows), :], final_nodes.at[aligned(plan[partners + i], rows), :])
            for i in range(blocks - partners)
        ],
        sems,
        2,
    )
    finish(copies)


def node_part(plan, returned, own, ready, front, first, second, gain, total, blocks):
    rows = returned[0].shape[0]
    total[...] = own[...]
    for i, block in enumerate(returned):
        total[aligned(plan[2 * blocks + i], rows), :] += block[...].astype(f32)
    width = front.shape[1]
    return node_update(front, ready[...], total[...], first[width:, :], second, gain)


def node_kernel(plan, flag, *refs):
    returned, refs = refs[:partners], refs[partners:]
    own, ready, front, first, second, gain, entering, new_one, new_two, total, sems = refs
    rows = returned[0].shape[0]
    blocks = entering.shape[0] // rows
    updated = node_part(
        plan, returned, own, ready, front, first, second, gain, total, blocks
    )
    half = new_one.shape[0]
    new_one[...] = updated[:half, :]
    new_two[...] = updated[half:, :]
    parts = [
        (i, (new_one, new_two)[i * rows // half], i % (half // rows)) for i in range(partners)
    ]

    @pl.when(flag[0] == 1)
    def _():
        finish(
            started(
                [
                    (entering.at[aligned(plan[i], rows), :], part.at[span(j, rows), :])
                    for i, part, j in parts
                ],
                sems,
            )
        )


def node_last_kernel(plan, *refs):
    returned, refs = refs[:partners], refs[partners:]
    own, ready, front, first, second, gain, _, final_nodes, total, near, sems = refs
    rows = returned[0].shape[0]
    blocks = final_nodes.shape[0] // rows
    near[...] = node_part(plan, returned, own, ready, front, first, second, gain, total, blocks)
    finish(
        started(
            [
                (near.at[span(i, rows), :], final_nodes.at[aligned(plan[i], rows), :])
                for i in range(partners)
            ],
            sems,
        )
    )


def ticks(
    node_latents,
    edge_latents,
    entering_nodes,
    entering_edges,
    edge_first,
    edge_second,
    edge_gain,
    node_first,
    node_second,
    node_gain,
    pair_list,
    send_list,
    senders,
    receivers,
):
    edge_second, node_first, node_second = edge_second[0], node_first[0], node_second[0]
    last = lax.axis_index("section") == lax.axis_size("section") - 1
    flag = last.astype(jnp.int32).reshape(1)
    here = lax.axis_index("dom").astype(jnp.int32).reshape(1)
    node_rows, width = entering_nodes.shape
    edge_rows = entering_edges.shape[0]
    rows = senders.shape[1]
    blocks = node_rows // rows
    number = edge_rows // rows
    one_rows = number // 2 * rows
    two_rows = edge_rows - one_rows
    kept, rest = partners * rows, node_rows - partners * rows
    square = 2 * width * width
    block = ("v", shape((rows, width), bf16))
    front_out = ("v", shape((kept, width), bf16))
    front_half = ("v", shape((kept // 2, width), bf16))
    back_out = ("v", shape((rest, width), bf16))
    one_low = ("v", shape((one_rows, width), bf16))
    two_low = ("v", shape((two_rows, width), bf16))
    one_wide = ("v", shape((one_rows, width), f32))
    two_wide = ("v", shape((two_rows, width), f32))
    weight = ("v", shape((width, width), bf16))
    all_low = ("v", shape((node_rows, width), bf16))
    slots = ("v", shape((node_rows + kept, width), f32))
    front_wide = ("v", shape((kept, width), f32))

    plan, nodes, *picked = call(
        plan_kernel,
        [("s", here), ("h", send_list), ("h", jnp.transpose(pair_list, (2, 0, 1))), ("h", node_latents[0])],
        [("s", shape((2 * blocks + partners + 2 * number,), jnp.int32)), all_low]
        + [block] * partners,
        scratch=[pltpu.SMEM((1, partners), jnp.int32), pltpu.SMEM((3, 1, number), jnp.int32)],
        copies=3,
        moved=1 << 20,
    )

    def fetched(picked):
        return [swapped(picked[i], *exchanges[i]) for i in range(partners)]

    def edge_stage(kernel, extra, incoming, base, sent, received, edges):
        new_one, new_two, low, sums, *partials = call(
            kernel,
            [("s", plan)]
            + extra
            + [("v", value) for value in (*incoming, *base, sent, received, ends, flipped)]
            + [("v", value) for value in (*edges, w_sent, edge_second, edge_gain)],
            [one_low, two_low, ("v", shape((edge_rows, width), bf16)), slots]
            + [block] * partners,
            scratch=[pltpu.VMEM((node_rows + kept, width), bf16)],
            copies=2 if extra else 0,
            flops=square * 2 * edge_rows,
            moved=16 << 20,
        )
        return (new_one, new_two), low, sums, partials

    def handed_back(partials):
        return [swapped(partials[i], *exchanges[i]) for i in range(partners)]

    incoming = fetched(picked)
    (
        front,
        back,
        edges_one,
        edges_two,
        w_edge,
        w_sent,
        w_received,
        base_one,
        base_two,
        sent,
        received,
        ends,
        flipped,
    ) = call(
        load_kernel,
        [("s", plan), ("v", nodes)]
        + [("h", value) for value in (edge_latents[0], edge_first[0], senders, receivers)],
        [front_out, back_out, one_low, two_low, weight, weight, weight, one_wide, two_wide]
        + [all_low, all_low]
        + [("v", shape((edge_rows, 2 * rows), bf16)), ("v", shape((2 * edge_rows, rows), bf16))],
        scratch=[pltpu.VMEM((edge_rows, rows), jnp.int32)] * 2,
        copies=7,
        flops=square * (edge_rows + 2 * node_rows),
        moved=16 << 20,
    )
    edges, low, sums, partials = edge_stage(
        edge_kernel,
        [("s", flag), ("h", entering_edges)],
        incoming,
        (base_one, base_two), sent, received, (edges_one, edges_two)
    )
    edges_one = passed_along(edges[0], "section", 1)
    returned = handed_back(partials)
    own, ready, new_back = call(
        settle_kernel,
        [("s", plan), ("s", flag)]
        + [
            ("v", value)
            for value in (low, flipped, sums, front, back, node_first, node_second, node_gain)
        ]
        + [("h", entering_nodes)],
        [front_wide, front_wide, back_out],
        scratch=[pltpu.VMEM((node_rows, width), f32)],
        copies=blocks - partners,
        flops=square * 2 * node_rows,
        moved=12 << 20,
    )
    back = passed_along(new_back, "section", 1)
    new_one, new_two = call(
        node_kernel,
        [("s", plan), ("s", flag)]
        + [
            ("v", value)
            for value in (*returned, own, ready, front, node_first, node_second, node_gain)
        ]
        + [("h", entering_nodes)],
        [front_half, front_half],
        scratch=[pltpu.VMEM((kept, width), f32)],
        copies=partners,
        flops=square * 2 * kept,
        moved=6 << 20,
    )
    front_one = passed_along(new_one, "section", 1)
    front_two = passed_along(new_two, "section", 1)
    edges_two = passed_along(edges[1], "section", 1)

    early = partners // 2
    picked = call(
        functools.partial(pick_kernel, 2 * blocks),
        [("s", plan), ("v", front_one)],
        [block] * early,
        moved=1 << 20,
    )
    front, *late = call(
        functools.partial(join_kernel, 2 * blocks),
        [("s", plan), ("v", front_one), ("v", front_two)],
        [front_out] + [block] * (partners - early),
        moved=2 << 20,
    )
    picked = [*picked, *late]
    incoming = fetched(picked)
    base_one, sent, received = call(
        project_kernel,
        [("v", value) for value in (front, back, edges_one, w_edge, w_sent, w_received)],
        [one_wide, all_low, all_low],
        flops=square * (one_rows + 2 * node_rows),
        moved=8 << 20,
    )
    (base_two,) = call(
        base_kernel,
        [("v", edges_two), ("v", w_edge)],
        [two_wide],
        flops=square * two_rows,
        moved=3 << 20,
    )
    edges, low, sums, partials = edge_stage(
        edge_last_kernel,
        [],
        incoming,
        (base_one, base_two), sent, received, (edges_one, edges_two)
    )
    returned = handed_back(partials)
    own, ready, final_nodes, final_edges = call(
        settle_last_kernel,
        [("s", plan)]
        + [
            ("v", value)
            for value in (low, flipped, sums, front, back, node_first, node_second, node_gain)
        ]
        + [("v", value) for value in edges],
        [front_wide, front_wide]
        + [("h", shape((node_rows, width), bf16)), ("h", shape((edge_rows, width), bf16))],
        scratch=[pltpu.VMEM((node_rows, width), f32), pltpu.VMEM((rest, width), bf16)],
        copies=2 + blocks - partners,
        flops=square * 2 * node_rows,
        moved=12 << 20,
    )
    (final_nodes,) = call(
        node_last_kernel,
        [("s", plan)]
        + [
            ("v", value)
            for value in (*returned, own, ready, front, node_first, node_second, node_gain)
        ]
        + [("h", final_nodes)],
        [("h", shape((node_rows, width), bf16))],
        scratch=[pltpu.VMEM((kept, width), f32), pltpu.VMEM((kept, width), bf16)],
        copies=partners,
        aliases={7 + partners: 0},
        flops=square * 2 * kept,
        moved=6 << 20,
    )
    return (final_nodes[None], final_edges[None])


def solution(mesh):
    placed = (
        P("section", "dom", None),
        P("section", "dom", None),
        P("dom", None),
        P("dom", None),
        P("section", None, None),
        P("section", None, None),
        P("section", None),
        P("section", None, None),
        P("section", None, None),
        P("section", None),
        P("dom", None, None),
        P("dom", None),
        P("dom", None),
        P("dom", None),
    )
    return jax.shard_map(
        ticks,
        mesh=mesh,
        in_specs=placed,
        out_specs=(P("section", "dom", None), P("section", "dom", None)),
        check_vma=False,
    )
```
